32 devices in a mesh: row: 16 (over z, y, core), col: 2 (over x).
Axes of the slice: x: 2, y: 2, z: 4, core: 2. Of those that a mesh axis runs over, the one named last changes fastest.
Arguments:
- seq: float32 [768, 1024], P('row', 'col'), may hold values from -6 to 6
- query: float32 [768, 1024], P('row', 'col'), may hold values from -24 to 24, as said below
- key: float32 [768, 1024], P('col', 'row'), may hold values from -24 to 24, as said below
- value: float32 [768, 1024], P('col', 'row'), may hold values from -6 to 6
- pair: float32 [768, 768, 128], P('row', 'col'), may hold values from -6 to 6
- w_bias: float32 [128, 32], replicated, may hold values from -0.5 to 0.5
- w_out: float32 [1024, 1024], P(None, 'col'), may hold values from -0.75 to 0.75
- w_left: float32 [1024, 64], P('col'), may hold values from -0.1875 to 0.1875
- w_right: float32 [1024, 64], P('col'), may hold values from -0.1875 to 0.1875
- w_outer: float32 [128, 128], replicated, may hold values from -0.5 to 0.5
- outer_bias: float32 [128], replicated, may hold values from -3 to 3
- w_up: float32 [128, 512], replicated, may hold values from -0.5 to 0.5
- w_down: float32 [512, 128], replicated, may hold values from -0.25 to 0.25
Outputs:
- seq_new: float32 [768, 1024], P('row', 'col')
- pair_new: float32 [768, 768, 128], P('row', 'col')
The draws below stay inside these ranges and needn't reach their ends.
Inputs may be any that keep to these rules, and one draw needn't show every extreme that they name: `query`: Head-major queries of order one; some residues may be much larger. `key`: Head-major keys of order one; some residues may be much larger.
All inputs are finite; a program needn't handle non-finite values.
Results may differ from the reference program's by a relative error of at most 0.0003.
Values sent between devices are 32-bit elements; how exact they have to be, the bound alone decides.
A program may use at most 128 MiB of HBM per device.

```python
import jax
import jax.numpy as jnp
from jax import lax

HEADS = 32
CP = 128
PAIR_HIDDEN = 512
OPD = 64
RES = 48
D = 1024
RESIDUES = 768
N_ROW = 16


def draw_shared(key):
    base = jax.random.fold_in(key, 77)
    first, second = jax.random.split(base, 2)
    queries = jnp.clip(jax.random.normal(first, (RESIDUES, D), jnp.float32), -6.0, 6.0)
    keys_drawn = jnp.clip(jax.random.normal(second, (RESIDUES, D), jnp.float32), -6.0, 6.0)
    return (queries, keys_drawn)


def draw_query(key, part):
    return draw_shared(key)[0]


def draw_key(key, part):
    return draw_shared(key)[1]


def block_levels(key, dims, shards, least, largest):
    def one(position, shards_of):
        steps = jax.random.uniform(jax.random.fold_in(jax.random.fold_in(key, 6), position), (shards_of,), jnp.float32, least / len(shards), largest / len(shards))
        return jnp.repeat(jnp.exp(steps), dims[position] // shards_of).reshape((-1,) + (1,) * (len(dims) - position - 1))

    gain = one(*shards[0])
    for cut in shards[1:]:
        gain = gain * one(*cut)
    return gain


def noise(own_key, extent, deviation, bound, shards=(), dtype=jnp.bfloat16):
    level = block_levels(own_key, extent, shards, -0.22, 0.18) if shards else 1.0
    drawn = jax.random.normal(own_key, extent, jnp.float32) * deviation * level
    return jnp.minimum(jnp.maximum(drawn, -bound), bound).astype(dtype)


def setup_inputs(seed: int = 0) -> dict:
    splits = jax.random.split(jax.random.key(seed), 14)
    seq = noise(splits[0], (RESIDUES, D), 1.0, 6.0, ((0, 16), (1, 2)), jnp.float32)
    query = draw_query(jax.random.fold_in(splits[13], 71), 0)
    key = draw_key(jax.random.fold_in(splits[13], 71), 0)
    value = noise(splits[3], (RESIDUES, D), 1.0, 6.0, ((0, 2), (1, 16)), jnp.float32)
    pair = noise(splits[4], (RESIDUES, RESIDUES, CP), 1.0, 6.0, ((0, 16), (1, 2)), jnp.float32)
    w_bias = noise(splits[5], (CP, HEADS), CP ** -0.5, 0.5, (), jnp.float32)
    w_out = noise(splits[6], (D, D), (D // 16) ** -0.5, 0.75, ((1, 2),), jnp.float32)
    w_left = noise(splits[7], (D, OPD), D ** -0.5, 0.1875, ((0, 2),), jnp.float32)
    w_right = noise(splits[8], (D, OPD), D ** -0.5, 0.1875, ((0, 2),), jnp.float32)
    w_outer = noise(splits[9], (2 * OPD, CP), (2 * OPD) ** -0.5, 0.5, (), jnp.float32)
    outer_bias = noise(splits[10], (CP,), 0.5, 3.0, (), jnp.float32)
    w_up = noise(splits[11], (CP, PAIR_HIDDEN), CP ** -0.5, 0.5, (), jnp.float32)
    w_down = noise(splits[12], (PAIR_HIDDEN, CP), PAIR_HIDDEN ** -0.5, 0.25, (), jnp.float32)
    return {"seq": seq, "query": query, "key": key, "value": value, "pair": pair, "w_bias": w_bias, "w_out": w_out, "w_left": w_left, "w_right": w_right, "w_outer": w_outer, "outer_bias": outer_bias, "w_up": w_up, "w_down": w_down}


HIGH = lax.Precision.HIGHEST

def channel_norm(x):
    centre = x - lax.optimization_barrier(jnp.mean(x, axis=-1, keepdims=True))
    return centre * lax.rsqrt(lax.optimization_barrier(jnp.mean(centre * centre, axis=-1, keepdims=True)) + 1e-05)

def reference(seq, query, key, value, pair, w_bias, w_out, w_left, w_right, w_outer, outer_bias, w_up, w_down):
    residues = seq.shape[0]
    heads = w_bias.shape[1]
    head_dim = seq.shape[1] // heads
    proj_width = w_left.shape[1]
    blocks = pair.reshape(N_ROW, RES, residues, pair.shape[2])

    def make_bias(block):
        return jnp.einsum('ijc,ch->ihj', channel_norm(block), w_bias, precision=HIGH)
    bias = lax.map(make_bias, blocks).reshape(residues, heads, residues)
    q_heads = query.reshape(residues, heads, head_dim)
    k_heads = key.reshape(residues, heads, head_dim)
    v_heads = value.reshape(residues, heads, head_dim)
    scores = jnp.einsum('ihd,jhd->ihj', q_heads, k_heads, precision=HIGH) / jnp.sqrt(jnp.float32(head_dim)) + bias
    weights = jax.nn.softmax(scores, axis=-1)
    attn = jnp.einsum('ihj,jhd->ihd', weights, v_heads, precision=HIGH).reshape(residues, heads * head_dim)
    seq_new = seq + jnp.dot(attn, w_out, precision=HIGH)
    mean_value = lax.optimization_barrier(jnp.mean(seq_new, axis=1, keepdims=True))
    mean_square = lax.optimization_barrier(jnp.mean(seq_new * seq_new, axis=1, keepdims=True))
    seq_norm = (seq_new - mean_value) * lax.rsqrt(mean_square - mean_value * mean_value + 1e-05)
    left = jnp.dot(seq_norm, w_left, precision=HIGH)
    right = jnp.dot(seq_norm, w_right, precision=HIGH)
    w_prod = w_outer[:proj_width]
    w_diff = w_outer[proj_width:]
    table = right[:, :, None] * w_prod[None, :, :]
    right_diff = jnp.dot(right, w_diff, precision=HIGH)
    left_diff = jnp.dot(left, w_diff, precision=HIGH)
    left_blocks = left.reshape(N_ROW, RES, proj_width)
    left_diff_blocks = left_diff.reshape(N_ROW, RES, left_diff.shape[1])

    def update(args):
        block, left_block, diff_block = args
        outer = jnp.einsum('ip,jpc->ijc', left_block, table, precision=HIGH) + diff_block[:, None, :] - right_diff[None, :, :] + outer_bias
        mid = block + outer
        hidden_act = jax.nn.relu(jnp.einsum('ijc,ck->ijk', channel_norm(mid), w_up, precision=HIGH))
        return mid + jnp.einsum('ijk,kc->ijc', hidden_act, w_down, precision=HIGH)
    pair_new = lax.map(update, (blocks, left_blocks, left_diff_blocks)).reshape(pair.shape)
    return (seq_new, pair_new)
```

```python
import functools

import jax
import jax.numpy as jnp
from jax import lax
from jax.experimental import pallas as pl
from jax.experimental.pallas import tpu as pltpu
from jax.sharding import PartitionSpec as P

HIGH = lax.Precision.HIGHEST
F32 = jnp.float32
BF16 = jnp.bfloat16
F8 = jnp.float8_e4m3fn
HIDDEN_SCALE = 2.0**11
DOWN_SCALE = 2.0**10
VMEM_LIMIT = 60 * 1024 * 1024
MESH = pl.DeviceIdType.MESH


def halves(x):
    high = x.astype(BF16)
    low = (x - high.astype(F32)).astype(BF16)
    return high, low


def channel_norm(x):
    centre = x - jnp.mean(x, axis=-1, keepdims=True)
    return centre * lax.rsqrt(jnp.mean(centre * centre, axis=-1, keepdims=True) + 1e-05)


def dot_nt(a, b, precision=None):
    return lax.dot_general(
        a, b, (((1,), (1,)), ((), ())), precision=precision, preferred_element_type=F32
    )


def split3(x):
    high = x.astype(BF16)
    rest = x - high.astype(F32)
    mid = rest.astype(BF16)
    low = (rest - mid.astype(F32)).astype(BF16)
    return high, mid, low


def sequence_kernel(
    n, n_col, head_dim, heads,
    kt_ref, vt_ref, q_ref, pair_ref, wbt_ref, seq_ref, w_out_ref, wlt_ref, wrt_ref,
    seq_out, left_out, right_out,
    k_buf, v_buf, q_buf, q_cat, bias_buf, pair_buf, rep_buf, wt_hi_ref, wt_lo_ref,
    w_out_buf, both_t, acc, msg, msg_in, sums, sums_in, packet, packet_in, right_mine, right_buf,
    recv_sem, z_sem, y_sem, core_sem, q_send, q_recv, pair_sem, load_sem,
    msg_send, msg_recv, sums_send, sums_recv, pack_send, pack_recv,
    right_send, right_recv, relay_send,
):
    n_z = n // 4
    feats, cols = kt_ref.shape
    rows, here = q_ref.shape
    width = w_out_ref.shape[0]
    proj = left_out.shape[1]
    groups, group = pair_buf.shape[:2]
    channels = pair_buf.shape[3]
    chip_heads = 2 * feats // head_dim
    wide = 2 * feats
    blocks = right_buf.shape[0]
    row, col = lax.axis_index("row"), lax.axis_index("col")
    core, y, z = lax.rem(row, 2), lax.rem(lax.div(row, 2), 2), lax.div(row, 4)
    core_peer, y_peer = row + 1 - 2 * core, row + 2 - 4 * y
    row_peers = [lax.rem(row + 2 * k, n) for k in range(1, n // 2)]
    col_peers = [lax.rem(col + k, n_col) for k in range(1, n_col)]
    signs = (1, -1)
    dot = functools.partial(jnp.dot, preferred_element_type=F32)

    def put(src, dst, send, recv, peer):
        return pltpu.make_async_remote_copy(
            src_ref=src, dst_ref=dst, send_sem=send, recv_sem=recv,
            device_id=peer, device_id_type=MESH,
        )

    def pair_copy(g):
        return pltpu.make_async_copy(
            pair_ref.at[pl.ds(g * group, group)], pair_buf.at[g], pair_sem.at[g]
        )

    bufs, owns = (k_buf, v_buf), (kt_ref, vt_ref)
    pair_copy(0).start()
    loads = [
        pltpu.make_async_copy(owns[kind], bufs[kind].at[row], recv_sem.at[row, kind])
        for kind in range(2)
    ]
    loads += [
        pltpu.make_async_copy(q_ref, q_buf.at[col], q_recv.at[col]),
        pltpu.make_async_copy(wlt_ref, both_t.at[:proj], load_sem.at[0]),
        pltpu.make_async_copy(wrt_ref, both_t.at[proj:], load_sem.at[1]),
        pltpu.make_async_copy(seq_ref, acc, load_sem.at[2]),
    ]
    for copy in loads:
        copy.start()
    for g in range(1, groups):
        pair_copy(g).start()
    load_w_out = pltpu.make_async_copy(w_out_ref, w_out_buf, load_sem.at[3])
    load_w_out.start()

    barrier = pltpu.get_barrier_semaphore()
    for peer in row_peers + [core_peer]:
        pl.semaphore_signal(barrier, inc=1, device_id={"row": peer}, device_id_type=MESH)
    for peer in col_peers:
        pl.semaphore_signal(barrier, inc=1, device_id={"col": peer}, device_id_type=MESH)
    pl.semaphore_wait(barrier, n // 2 + n_col - 1)

    def send_slot(src, kind, slot, sem, peer):
        return put(src, bufs[kind].at[slot], sem, recv_sem.at[slot, kind], {"row": peer})

    def inside(place):
        return jnp.logical_and(place >= 0, place < n_z)

    def own_sends(kind, act):
        for s, sign in enumerate(signs):

            @pl.when(inside(z + sign))
            def _():
                act(send_slot(owns[kind], kind, row, z_sem.at[0, s, kind], row + 4 * sign))

        act(send_slot(owns[kind], kind, row, y_sem.at[0, 0, kind], y_peer))
        act(send_slot(owns[kind], kind, row, core_sem.at[0, 0, 0, kind], core_peer))

    def line_sends(d, kind, act, wait):
        for s, sign in enumerate(signs):

            @pl.when(inside(z + sign * d))
            def _():
                slot = row + 4 * sign * d
                src = bufs[kind].at[slot]
                if wait:
                    send_slot(src, kind, slot, y_sem.at[d, s, kind], y_peer).wait_recv()

                @pl.when(inside(z - sign))
                def _():
                    act(send_slot(src, kind, slot, z_sem.at[d, s, kind], row - 4 * sign))

                act(send_slot(src, kind, slot, y_sem.at[d, s, kind], y_peer))
                act(send_slot(src, kind, slot, core_sem.at[d, s, 0, kind], core_peer))

    def cross_sends(d, kind, act, wait):
        for s, sign in enumerate(signs[: 1 if d == 0 else 2]):

            @pl.when(inside(z + sign * d))
            def _():
                slot = y_peer + 4 * sign * d
                src = bufs[kind].at[slot]
                copy = send_slot(src, kind, slot, core_sem.at[d, s, 1, kind], core_peer)
                if wait:
                    copy.wait_recv()
                act(copy)

    start = lambda copy: copy.start()
    wait_send = lambda copy: copy.wait_send()

    def q_copy(k, source):
        return put(
            q_ref, q_buf.at[source], q_send.at[k], q_recv.at[source], {"col": col_peers[k]}
        )

    own_sends(0, start)
    for k in range(n_col - 1):
        q_copy(k, col).start()
    own_sends(1, start)
    for copy in loads:
        copy.wait()

    both_hi, both_lo = halves(both_t[...])
    ones = jnp.ones((8, here), BF16)
    sums[...] = dot_nt(ones, both_hi) + dot_nt(ones, both_lo)
    sum_copies = [
        put(sums, sums_in.at[k], sums_send.at[k], sums_recv.at[k], {"col": peer})
        for k, peer in enumerate(col_peers)
    ]

    for h in range(heads):
        rep_buf[h * group : (h + 1) * group] = jnp.broadcast_to(
            wbt_ref[h : h + 1, :], (group, channels)
        )
    place = lax.rem(lax.broadcasted_iota(jnp.int32, rep_buf.shape, 0), group)
    for i in range(group):
        high, low = halves(jnp.where(place == i, rep_buf[...], 0.0))
        wt_hi_ref[:, i * channels : (i + 1) * channels] = high
        wt_lo_ref[:, i * channels : (i + 1) * channels] = low
    for copy in sum_copies:
        copy.start()

    def bias_group(g, carry):
        pair_copy(g).wait()
        parts = [halves(channel_norm(pair_buf[g, i])) for i in range(group)]
        high = jnp.concatenate([p[0] for p in parts], axis=1)
        low = jnp.concatenate([p[1] for p in parts], axis=1)
        wt_hi = wt_hi_ref[...]
        flat = dot_nt(wt_hi, high) + (dot_nt(wt_hi, low) + dot_nt(wt_lo_ref[...], high))
        bias_buf[:, pl.ds(pl.multiple_of(g * group, group), group), :] = flat.reshape(
            heads, group, flat.shape[1]
        )
        return carry

    def bias_groups(part):
        lax.fori_loop(part * groups // 3, (part + 1) * groups // 3, bias_group, 0)

    tile = 128
    tile_heads = tile // head_dim
    per_col = here // tile
    scale = F32(head_dim) ** -0.5

    def spread_queries(index, carry):
        at = pl.multiple_of(lax.rem(index, per_col) * tile, tile)
        q = q_buf[lax.div(index, per_col), :, pl.ds(at, tile)] * scale
        turns = [q] + [pltpu.roll(q, m * head_dim, 1) for m in range(1, tile_heads)]
        lane = lax.broadcasted_iota(jnp.int32, q.shape, 1) // head_dim
        for m in range(tile_heads):
            every = turns[(0 - m) % tile_heads]
            for p in range(1, tile_heads):
                every = jnp.where(lane == p, turns[(p - m) % tile_heads], every)
            high, mid, low = [part.astype(F32) for part in split3(every)]
            first = jnp.where(lane == 2, mid, high).astype(BF16)
            second = jnp.where(lane == 0, mid, low).astype(BF16)
            q_cat[index * tile_heads + m] = jnp.concatenate(
                [first, second[:, : 2 * head_dim]], axis=1
            )
        return carry

    def event(d, kind):
        line_sends(d, kind, start, True)
        cross_sends(d - 1, kind, start, True)

    lane = lax.broadcasted_iota(jnp.int32, (rows, wide), 1)
    head_lane = lane // head_dim
    upper = lax.rem(lane, head_dim) >= head_dim // 2

    def msg_copies(chip):
        return [
            put(
                msg.at[chip], msg_in.at[k, chip], msg_send.at[k, chip], msg_recv.at[k, chip],
                {"col": peer},
            )
            for k, peer in enumerate(col_peers)
        ]

    def order(t):
        out = jnp.int32(0)
        for here_z in range(n_z):
            up_first = here_z < n_z - 1 - here_z
            ranked = sorted(
                range(n_z),
                key=lambda a: (abs(a - here_z), (a < here_z) if up_first else (a > here_z)),
            )
            out = out + ranked[t] * (z == here_z).astype(jnp.int32)
        return out

    def chip_at(t, u):
        return 2 * order(t) + y + u * (1 - 2 * y)

    def attend(t, u):
        chip = chip_at(t, u)
        base = 2 * chip
        other = base + 1 - core
        for kind in range(2):
            put(
                bufs[kind].at[other], bufs[kind].at[other], core_sem.at[0, 0, 0, kind],
                recv_sem.at[other, kind], {"row": core_peer},
            ).wait_recv()
        keys = k_buf[pl.ds(base, 2)].reshape(wide, cols)
        values = v_buf[pl.ds(base, 2)].reshape(wide, cols)
        k_hi, k_mid, k_lo = split3(keys)
        expos, part_stat = [], jnp.zeros((rows, wide), F32)
        for m in range(chip_heads):
            mine = slice(m * head_dim, (m + 1) * head_dim)
            a, b, c = k_hi[mine], k_mid[mine], k_lo[mine]
            head = chip * chip_heads + m
            stacked = jnp.concatenate([a, b, a, c, b, a], axis=0)
            scores = dot(q_cat[head], stacked) + bias_buf[head]
            top = jnp.max(scores, axis=1, keepdims=True)
            expo = jnp.exp(scores - top)
            total = jnp.sum(expo, axis=1, keepdims=True)
            expos.append(expo)
            part_stat = jnp.where(head_lane == m, jnp.where(upper, total, top), part_stat)
        e_hi, e_lo = halves(jnp.concatenate(expos, axis=0))
        v_hi, v_lo = halves(values)
        out = dot_nt(e_hi, v_hi) + (dot_nt(e_hi, v_lo) + dot_nt(e_lo, v_hi))
        part = out[:rows]
        for m in range(1, chip_heads):
            part = jnp.where(head_lane == m, out[m * rows : (m + 1) * rows], part)
        msg[chip, :rows] = part
        msg[chip, rows:] = part_stat
        for copy in msg_copies(chip):
            copy.start()

    def combine(t, u):
        chip = chip_at(t, u)
        for copy in msg_copies(chip):
            copy.wait()
        every = [msg[chip]] + [msg_in[k, chip] for k in range(n_col - 1)]
        stats = [e[rows:] for e in every]
        down = [pltpu.roll(s, wide - head_dim // 2, 1) for s in stats]
        up = [pltpu.roll(s, head_dim // 2, 1) for s in stats]
        tops = [jnp.where(upper, r, s) for s, r in zip(stats, up)]
        totals = [jnp.where(upper, s, r) for s, r in zip(stats, down)]
        highest = functools.reduce(jnp.maximum, tops)
        scales = [jnp.exp(top - highest) for top in tops]
        total = sum(s * t for s, t in zip(scales, totals))
        attn = sum(e[:rows] * s for e, s in zip(every, scales)) / total
        a_hi, a_lo = halves(attn)
        at = pl.multiple_of(chip * wide, wide)
        w_hi, w_lo = halves(w_out_buf[pl.ds(at, wide), :])
        acc[...] += dot(a_hi, w_hi) + (dot(a_hi, w_lo) + dot(a_lo, w_hi))

    def stage(t):
        def one(u, carry):
            attend(t, u)
            if t:
                combine(t - 1, u)
            return carry

        lax.fori_loop(0, 2, one, 0)

    bias_groups(0)
    event(1, 0)
    bias_groups(1)
    event(1, 1)
    bias_groups(2)
    for k in range(1, n_col):
        source = lax.rem(col - k + n_col, n_col)
        q_copy(k - 1, source).wait_recv()
    lax.fori_loop(0, heads // tile_heads, spread_queries, 0)
    load_w_out.wait()
    for d in range(2, n_z):
        event(d, 0)
        stage(d - 2)
        event(d, 1)
    stage(n_z - 2)
    attend(n_z - 1, 0)
    combine(n_z - 2, 0)
    for kind in range(2):
        cross_sends(n_z - 1, kind, start, True)
    attend(n_z - 1, 1)
    combine(n_z - 2, 1)
    for copy in sum_copies:
        copy.wait()
    for u in range(2):
        combine(n_z - 1, u)

    seq_new = acc[...]
    seq_out[...] = seq_new
    local_mean = jnp.mean(seq_new, axis=1, keepdims=True)
    centred = seq_new - local_mean
    spread = jnp.sum(centred * centred, axis=1, keepdims=True)
    both_hi, both_lo = halves(both_t[...])
    c_hi, c_lo = halves(centred)
    packet[:rows] = dot_nt(c_hi, both_hi) + (dot_nt(c_hi, both_lo) + dot_nt(c_lo, both_hi))
    wide_lane = lax.broadcasted_iota(jnp.int32, (rows, 2 * proj), 1)
    packet[rows:] = jnp.where(wide_lane < proj, local_mean, spread)
    packets = [
        put(packet, packet_in.at[k], pack_send.at[k], pack_recv.at[k], {"col": peer})
        for k, peer in enumerate(col_peers)
    ]
    for copy in packets:
        copy.start()
    for copy in packets:
        copy.wait()
    every = [packet[...]] + [packet_in[k] for k in range(n_col - 1)]
    weights = [sums[:1]] + [sums_in[k, :1] for k in range(n_col - 1)]
    means = [p[rows:, :1] for p in every]
    mean = sum(means) / n_col
    offsets = [m - mean for m in means]
    variance = (
        sum(p[rows:, proj : proj + 1] for p in every) + here * sum(o * o for o in offsets)
    ) / width
    both = sum(p[:rows] + o * w for p, o, w in zip(every, offsets, weights))
    both = both * lax.rsqrt(variance + 1e-05)
    left_out[...] = both[:, :proj]
    half = rows // 2
    right_mine[...] = jnp.concatenate([both[:half, proj:], both[half:, proj:]], axis=1)

    mine = lax.div(row, blocks) == col
    own = lax.rem(row, blocks)

    def row_copies():
        return [
            put(
                right_mine, right_buf.at[own], right_send.at[k], right_recv.at[own],
                {"row": peer},
            )
            for k, peer in enumerate(row_peers)
        ]

    @pl.when(mine)
    def _():
        for copy in row_copies():
            copy.start()
        keep = pltpu.make_async_copy(right_mine, right_buf.at[own], right_recv.at[own])
        keep.start()
        keep.wait()

    def relay(j, block):
        slot = right_buf.at[block]
        return put(slot, slot, relay_send.at[j], right_recv.at[block], {"row": core_peer})

    for j in range(blocks // 2):
        block = 2 * j + core

        @pl.when(col * blocks + block != row)
        def _():
            relay(j, block).wait_recv()

        relay(j, block).start()
    for j in range(blocks // 2):
        relay(j, 2 * j + 1 - core).wait_recv()
    for b in range(blocks):
        packed = right_buf[b]
        right_out[b * rows : b * rows + half] = packed[:, :proj]
        right_out[b * rows + half : (b + 1) * rows] = packed[:, proj:]

    for j in range(blocks // 2):
        relay(j, 2 * j + core).wait_send()

    @pl.when(mine)
    def _():
        for copy in row_copies():
            copy.wait_send()

    for kind in range(2):
        own_sends(kind, wait_send)
        for d in range(1, n_z):
            line_sends(d, kind, wait_send, False)
        for d in range(n_z):
            cross_sends(d, kind, wait_send, False)
    for k in range(n_col - 1):
        q_copy(k, col).wait_send()


def sequence_update(seq, query, key, value, pair, w_bias, w_out, w_left, w_right):
    n, n_col = lax.axis_size("row"), lax.axis_size("col")
    rows, cols, channels = pair.shape
    heads = w_bias.shape[1]
    feats = key.shape[1]
    width, here = w_out.shape
    head_dim = width // heads
    proj = w_left.shape[1]
    blocks = cols // rows
    group = 8
    peers = n_col - 1
    n_z = n // 4
    chips = n // 2
    any_space = pl.BlockSpec(memory_space=pl.ANY)
    vmem = pl.BlockSpec(memory_space=pltpu.VMEM)
    dma = pltpu.SemaphoreType.DMA
    return pl.pallas_call(
        functools.partial(sequence_kernel, n, n_col, head_dim, heads),
        out_shape=(
            jax.ShapeDtypeStruct(seq.shape, F32),
            jax.ShapeDtypeStruct((rows, proj), F32),
            jax.ShapeDtypeStruct((cols, proj), F32),
        ),
        in_specs=[any_space] * 4 + [vmem] + [any_space] * 4,
        out_specs=(vmem,) * 3,
        scratch_shapes=[
            pltpu.VMEM((n, feats, cols), F32),
            pltpu.VMEM((n, feats, cols), F32),
            pltpu.VMEM((n_col, rows, here), F32),
            pltpu.VMEM((heads, rows, 6 * head_dim), BF16),
            pltpu.VMEM((heads, rows, cols), F32),
            pltpu.VMEM((rows // group, group, cols, channels), F32),
            pltpu.VMEM((heads * group, channels), F32),
            pltpu.VMEM((heads * group, group * channels), BF16),
            pltpu.VMEM((heads * group, group * channels), BF16),
            pltpu.VMEM((width, here), F32),
            pltpu.VMEM((2 * proj, here), F32),
            pltpu.VMEM((rows, here), F32),
            pltpu.VMEM((chips, 2 * rows, 2 * feats), F32),
            pltpu.VMEM((peers, chips, 2 * rows, 2 * feats), F32),
            pltpu.VMEM((8, 2 * proj), F32),
            pltpu.VMEM((peers, 8, 2 * proj), F32),
            pltpu.VMEM((2 * rows, 2 * proj), F32),
            pltpu.VMEM((peers, 2 * rows, 2 * proj), F32),
            pltpu.VMEM((rows // 2, 2 * proj), F32),
            pltpu.VMEM((blocks, rows // 2, 2 * proj), F32),
            dma((n, 2)), dma((n_z, 2, 2)), dma((n_z, 2, 2)), dma((n_z, 2, 2, 2)),
            dma((peers,)), dma((n_col,)), dma((rows // group,)), dma((4,)),
            dma((peers, chips)), dma((peers, chips)), dma((peers,)), dma((peers,)),
            dma((peers,)), dma((peers,)),
            dma((n // 2 - 1,)), dma((blocks,)), dma((blocks // 2,)),
        ],
        compiler_params=pltpu.CompilerParams(
            vmem_limit_bytes=VMEM_LIMIT, collective_id=0, has_side_effects=True
        ),
        name="sequence_update",
    )(key.T, value.T, query, pair, w_bias.T, seq, w_out, w_left.T, w_right.T)


def transition_kernel(
    pair_ref, left_ref, right_ref, w_outer_ref, bias_ref, w_up_ref, w_down_ref, seq_ref,
    seq_out, out_ref,
    left_t, right_s, left_d, up_ref, up8_ref, down_ref, down8_ref,
):
    step = pl.program_id(0)
    group, cols, channels = pair_ref.shape
    proj = left_ref.shape[1]
    dot = functools.partial(jnp.dot, preferred_element_type=F32)

    @pl.when(step == 0)
    def _():
        seq_out[...] = seq_ref[...]
        left = left_ref[...]
        left_t[...] = left.T
        left_d[...] = jnp.dot(left, w_outer_ref[proj:], precision=HIGH) + bias_ref[...]
        r_hi, r_lo = halves(right_ref[...])
        right_s[...] = jnp.concatenate([r_hi, r_lo, r_hi], axis=1)
        up = w_up_ref[...] * HIDDEN_SCALE
        up_hi = up.astype(BF16)
        up_ref[...] = jnp.concatenate([up_hi, up_hi], axis=0)
        up8_ref[...] = (up - up_hi.astype(F32)).astype(F8)
        down = w_down_ref[...] * (1.0 / HIDDEN_SCALE)
        down_hi, down_lo = halves(down)
        down_ref[...] = jnp.concatenate([down_hi, down_lo], axis=1)
        down8_ref[...] = (w_down_ref[...] * DOWN_SCALE).astype(F8)

    lane = lax.broadcasted_iota(jnp.int32, left_t.shape, 1)
    w_prod = w_outer_ref[:proj]
    w_diff = w_outer_ref[proj:]
    weights = []
    for g in range(group):
        column = jnp.sum(
            jnp.where(lane == step * group + g, left_t[...], 0.0), axis=1, keepdims=True
        )
        w_hi, w_lo = halves(column * w_prod - w_diff)
        weights.append(jnp.concatenate([w_hi, w_hi, w_lo], axis=0))
    outer = dot(right_s[...], jnp.concatenate(weights, axis=1))
    for first in range(0, group, 2):
        pick = range(first, first + 2)
        mids = [
            pair_ref[g]
            + (
                outer[:, g * channels : (g + 1) * channels]
                + left_d[pl.ds(step * group + g, 1), :]
            )
            for g in pick
        ]
        xs = [channel_norm(mid) for mid in mids]
        pairs = [jnp.concatenate(halves(x), axis=1) for x in xs]
        main = [dot(x, up_ref[...]) for x in pairs]
        rest = [dot(x.astype(F8), up8_ref[...]) for x in xs]
        hidden = [jnp.maximum(m + r, 0.0) for m, r in zip(main, rest)]
        highs = [h.astype(BF16) for h in hidden]
        lows = [(h - high.astype(F32)).astype(F8) for h, high in zip(hidden, highs)]
        both = [dot(high, down_ref[...]) for high in highs]
        rest = [dot(low, down8_ref[...]) * (1.0 / (HIDDEN_SCALE * DOWN_SCALE)) for low in lows]
        for g, mid, b, r in zip(pick, mids, both, rest):
            out_ref[g] = mid + (b[:, :channels] + (b[:, channels:] + r))


def transition(pair, left, right, w_outer, outer_bias, w_up, w_down, seq_new):
    rows, cols, channels = pair.shape
    proj = left.shape[1]
    hidden = w_up.shape[1]
    group = 4

    def whole(x):
        return pl.BlockSpec(x.shape, lambda i: (0,) * x.ndim)

    block = pl.BlockSpec((group, cols, channels), lambda i: (i, 0, 0))
    fixed = (left, right, w_outer, outer_bias.reshape(1, channels), w_up, w_down, seq_new)
    return pl.pallas_call(
        transition_kernel,
        out_shape=(
            jax.ShapeDtypeStruct(seq_new.shape, F32),
            jax.ShapeDtypeStruct(pair.shape, F32),
        ),
        grid=(rows // group,),
        in_specs=[block] + [whole(x) for x in fixed],
        out_specs=(whole(seq_new), block),
        scratch_shapes=[
            pltpu.VMEM((proj, rows), F32),
            pltpu.VMEM((cols, 3 * proj), BF16),
            pltpu.VMEM((rows, channels), F32),
            pltpu.VMEM((2 * channels, hidden), BF16),
            pltpu.VMEM((channels, hidden), F8),
            pltpu.VMEM((hidden, 2 * channels), BF16),
            pltpu.VMEM((hidden, channels), F8),
        ],
        compiler_params=pltpu.CompilerParams(vmem_limit_bytes=VMEM_LIMIT),
        name="transition",
    )(pair, *fixed)


def per_device(
    seq, query, key, value, pair, w_bias, w_out, w_left, w_right, w_outer, outer_bias, w_up, w_down
):
    seq_new, left, right = sequence_update(
        seq, query, key, value, pair, w_bias, w_out, w_left, w_right
    )
    return transition(pair, left, right, w_outer, outer_bias, w_up, w_down, seq_new)


def solution(mesh):
    in_specs = (
        P("row", "col"),
        P("row", "col"),
        P("col", "row"),
        P("col", "row"),
        P("row", "col", None),
        P(),
        P(None, "col"),
        P("col", None),
        P("col", None),
        P(),
        P(),
        P(),
        P(),
    )
    out_specs = (P("row", "col"), P("row", "col", None))
    return jax.shard_map(
        per_device, mesh=mesh, in_specs=in_specs, out_specs=out_specs, check_vma=False
    )
```

```python
import functools

import jax
import jax.numpy as jnp
from jax import lax
from jax.experimental import pallas as pl
from jax.experimental.pallas import tpu as pltpu
from jax.sharding import PartitionSpec as P

HIGH = lax.Precision.HIGHEST
F32 = jnp.float32
BF16 = jnp.bfloat16
F8 = jnp.float8_e4m3fn
HIDDEN_SCALE = 2.0**11
DOWN_SCALE = 2.0**10
VMEM_LIMIT = 60 * 1024 * 1024
LANES = 128
MESH = pl.DeviceIdType.MESH


def halves(x):
    high = x.astype(BF16)
    low = (x - high.astype(F32)).astype(BF16)
    return high, low


def channel_norm(x):
    centre = x - jnp.mean(x, axis=-1, keepdims=True)
    return centre * lax.rsqrt(jnp.mean(centre * centre, axis=-1, keepdims=True) + 1e-05)


def dot_nt(a, b, precision=None):
    return lax.dot_general(
        a, b, (((1,), (1,)), ((), ())), precision=precision, preferred_element_type=F32
    )


def split3(x):
    high = x.astype(BF16)
    rest = x - high.astype(F32)
    mid = rest.astype(BF16)
    low = (rest - mid.astype(F32)).astype(BF16)
    return high, mid, low


def sequence_kernel(
    n, n_col, head_dim, heads,
    kt_ref, vt_ref, q_ref, pair_ref, wbt_ref, seq_ref, w_out_ref, wlt_ref, wrt_ref,
    seq_out, left_out, right_out,
    k_buf, v_buf, q_buf, q_cat, bias_buf, pair_buf, wt_ref,
    w_out_buf, both_t, acc, msg, msg_in, sums, sums_in, packet, packet_in, right_mine, right_buf,
    recv_sem, z_sem, y_sem, core_sem, around_sem, q_send, q_recv, pair_sem, load_sem,
    msg_send, msg_recv, sums_send, sums_recv, pack_send, pack_recv,
    right_send, right_recv, relay_send,
):
    n_z = n // 4
    feats, cols = kt_ref.shape
    rows, here = q_ref.shape
    width = w_out_ref.shape[0]
    proj = left_out.shape[1]
    groups, group = pair_buf.shape[:2]
    channels = pair_buf.shape[3]
    chip_heads = 2 * feats // head_dim
    wide = 2 * feats
    blocks = right_buf.shape[0]
    bias_tiles = bias_buf.shape[0]
    row, col = lax.axis_index("row"), lax.axis_index("col")
    core, y, z = lax.rem(row, 2), lax.rem(lax.div(row, 2), 2), lax.div(row, 4)
    core_peer, y_peer = row + 1 - 2 * core, row + 2 - 4 * y
    row_peers = [lax.rem(row + 2 * k, n) for k in range(1, n // 2)]
    col_peers = [lax.rem(col + k, n_col) for k in range(1, n_col)]
    signs = (1, -1)
    dot = functools.partial(jnp.dot, preferred_element_type=F32)

    def put(src, dst, send, recv, peer):
        return pltpu.make_async_remote_copy(
            src_ref=src, dst_ref=dst, send_sem=send, recv_sem=recv,
            device_id=peer, device_id_type=MESH,
        )

    def pair_copy(g):
        return pltpu.make_async_copy(
            pair_ref.at[pl.ds(g * group, group)], pair_buf.at[g], pair_sem.at[g]
        )

    def inside(place):
        return jnp.logical_and(place >= 0, place < n_z)

    barrier = pltpu.get_barrier_semaphore()

    def greet(peer):
        pl.semaphore_signal(barrier, inc=1, device_id=peer, device_id_type=MESH)

    for sign in signs:

        @pl.when(inside(z + sign))
        def _():
            greet({"row": row + 4 * sign})

    for peer in (y_peer, core_peer):
        greet({"row": peer})
    for peer in col_peers:
        greet({"col": peer})

    bufs, owns = (k_buf, v_buf), (kt_ref, vt_ref)
    loads = [
        pltpu.make_async_copy(owns[kind], bufs[kind].at[row], recv_sem.at[row, kind])
        for kind in range(2)
    ]
    loads += [
        pltpu.make_async_copy(q_ref, q_buf.at[col], q_recv.at[col]),
        pltpu.make_async_copy(wlt_ref, both_t.at[:proj], load_sem.at[0]),
        pltpu.make_async_copy(wrt_ref, both_t.at[proj:], load_sem.at[1]),
        pltpu.make_async_copy(seq_ref, acc, load_sem.at[2]),
    ]
    for copy in loads:
        copy.start()
    neighbours = sum(inside(z + sign).astype(jnp.int32) for sign in signs)
    pl.semaphore_wait(barrier, neighbours + 2 + len(col_peers))

    def send_slot(src, kind, slot, sem, peer):
        return put(src, bufs[kind].at[slot], sem, recv_sem.at[slot, kind], {"row": peer})

    def at_end(place):
        return place < -99

    def own_sends(kind, act):
        for s, sign in enumerate(signs):

            @pl.when(inside(z + sign))
            def _():
                act(send_slot(bufs[kind].at[row], kind, row, z_sem.at[0, s, kind], row + 4 * sign))

        act(send_slot(bufs[kind].at[row], kind, row, y_sem.at[0, 0, kind], y_peer))
        act(send_slot(bufs[kind].at[row], kind, row, core_sem.at[0, 0, 0, kind], core_peer))

    def line_sends(d, kind, act, wait):
        for s, sign in enumerate(signs):

            @pl.when(inside(z + sign * d))
            def _():
                slot = row + 4 * sign * d
                src = bufs[kind].at[slot]
                if wait:
                    send_slot(src, kind, slot, y_sem.at[d, s, kind], y_peer).wait_recv()

                @pl.when(inside(z - sign))
                def _():
                    act(send_slot(src, kind, slot, z_sem.at[d, s, kind], row - 4 * sign))

                if kind == 0:
                    act(send_slot(src, kind, slot, y_sem.at[d, s, kind], y_peer))
                else:

                    @pl.when(jnp.logical_not(at_end(z + sign * d)))
                    def _():
                        act(send_slot(src, kind, slot, y_sem.at[d, s, kind], y_peer))

                act(send_slot(src, kind, slot, core_sem.at[d, s, 0, kind], core_peer))

    def cross_sends(d, kind, act, wait):
        for s, sign in enumerate(signs[: 1 if d == 0 else 2]):
            source = z + sign * d
            by_y = inside(source)
            if kind and d:
                by_y = jnp.logical_and(by_y, jnp.logical_not(at_end(source)))

            @pl.when(by_y)
            def _():
                slot = y_peer + 4 * sign * d
                src = bufs[kind].at[slot]
                copy = send_slot(src, kind, slot, core_sem.at[d, s, 1, kind], core_peer)
                if wait:
                    copy.wait_recv()
                act(copy)

    def around_sends(d, act, wait):
        for s, sign in enumerate(signs):
            source = z + sign * d

            @pl.when(jnp.logical_and(inside(source), at_end(source)))
            def _():
                slot = y_peer + 4 * sign * d
                src = v_buf.at[slot]
                if d:
                    copy = send_slot(src, 1, slot, core_sem.at[d, s, 1, 1], core_peer)
                    if wait:
                        copy.wait_recv()

                @pl.when(inside(z - sign))
                def _():
                    act(send_slot(src, 1, slot, around_sem.at[d, s], row - 4 * sign))

                if d:
                    act(copy)

    start = lambda copy: copy.start()
    wait_send = lambda copy: copy.wait_send()

    def q_copy(k, source):
        return put(
            q_ref, q_buf.at[source], q_send.at[k], q_recv.at[source], {"col": col_peers[k]}
        )

    loads[0].wait()
    own_sends(0, start)
    for k in range(n_col - 1):
        q_copy(k, col).start()
    loads[1].wait()
    own_sends(1, start)
    for g in range(groups):
        pair_copy(g).start()
    load_w_out = pltpu.make_async_copy(w_out_ref, w_out_buf, load_sem.at[3])
    load_w_out.start()
    for copy in loads[2:]:
        copy.wait()

    both_hi, both_lo = halves(both_t[...])
    ones = jnp.ones((8, here), BF16)
    sums[...] = dot_nt(ones, both_hi) + dot_nt(ones, both_lo)
    sum_copies = [
        put(sums, sums_in.at[k], sums_send.at[k], sums_recv.at[k], {"col": peer})
        for k, peer in enumerate(col_peers)
    ]

    wb_hi, wb_lo = halves(wbt_ref[...])
    wt_ref[:heads] = jnp.concatenate([wb_hi, wb_hi], axis=1)
    wt_ref[heads:] = jnp.concatenate([wb_lo, jnp.zeros_like(wb_lo)], axis=1)
    for copy in sum_copies:
        copy.start()

    def bias_group(g, carry):
        pair_copy(g).wait()
        for i in range(group):
            x = jnp.concatenate(halves(channel_norm(pair_buf[g, i])), axis=1)
            flat = dot_nt(wt_ref[...], x)
            flat = flat[:heads] + flat[heads:]
            if bias_tiles * LANES > cols:
                spare = jnp.zeros((heads, bias_tiles * LANES - cols), F32)
                flat = jnp.concatenate([flat, spare], axis=1)
            for j in range(bias_tiles):
                bias_buf[j, pl.ds(g * group + i, heads, stride=rows), :] = flat[
                    :, j * LANES : (j + 1) * LANES
                ]
        return carry

    tile = 128
    tile_heads = tile // head_dim
    per_col = here // tile
    scale = F32(head_dim) ** -0.5

    def spread_queries(index, carry):
        at = pl.multiple_of(lax.rem(index, per_col) * tile, tile)
        q = q_buf[lax.div(index, per_col), :, pl.ds(at, tile)] * scale
        turns = [q] + [pltpu.roll(q, m * head_dim, 1) for m in range(1, tile_heads)]
        lane = lax.broadcasted_iota(jnp.int32, q.shape, 1) // head_dim
        for m in range(tile_heads):
            every = turns[(0 - m) % tile_heads]
            for p in range(1, tile_heads):
                every = jnp.where(lane == p, turns[(p - m) % tile_heads], every)
            high, mid, low = [part.astype(F32) for part in split3(every)]
            first = jnp.where(lane == 2, mid, high).astype(BF16)
            second = jnp.where(lane == 0, mid, low).astype(BF16)
            q_cat[index * tile_heads + m] = jnp.concatenate(
                [first, second[:, : 2 * head_dim]], axis=1
            )
        return carry

    def event(d, kind):
        line_sends(d, kind, start, True)
        if kind == 0 and d > 1:
            around_sends(d - 1, start, True)
        cross_sends(d - 1, kind, start, True)
        if kind and d == 1:
            around_sends(0, start, True)

    lane = lax.broadcasted_iota(jnp.int32, (rows, wide), 1)
    head_lane = lane // head_dim
    upper = lax.rem(lane, head_dim) >= head_dim // 2

    def msg_copies(chip, part):
        at = pl.ds(part * rows, rows)
        return [
            put(
                msg.at[chip, at], msg_in.at[k, chip, at],
                msg_send.at[k, chip, part], msg_recv.at[k, chip, part], {"col": peer},
            )
            for k, peer in enumerate(col_peers)
        ]

    def order(t):
        out = jnp.int32(0)
        for here_z in range(n_z):
            up_first = here_z < n_z - 1 - here_z
            ranked = sorted(
                range(n_z),
                key=lambda a: (abs(a - here_z), (a < here_z) if up_first else (a > here_z)),
            )
            out = out + ranked[t] * (z == here_z).astype(jnp.int32)
        return out

    def chip_at(t, u):
        return 2 * order(t) + y + u * (1 - 2 * y)

    def bias_of(head):
        at = pl.ds(pl.multiple_of(head * rows, 8), rows)
        tiles = [bias_buf[j, at, :] for j in range(bias_tiles)]
        return jnp.concatenate(tiles, axis=1)[:, :cols]

    def await_other(chip, kind):
        other = 2 * chip + 1 - core
        put(
            bufs[kind].at[other], bufs[kind].at[other], core_sem.at[0, 0, 0, kind],
            recv_sem.at[other, kind], {"row": core_peer},
        ).wait_recv()

    def attend_keys(t, u):
        chip = chip_at(t, u)
        await_other(chip, 0)
        keys = k_buf[pl.ds(2 * chip, 2)].reshape(wide, cols)
        k_hi, k_mid, k_lo = split3(keys)
        expos, stat = [], jnp.zeros((rows, wide), F32)
        for m in range(chip_heads):
            mine = slice(m * head_dim, (m + 1) * head_dim)
            a, b, c = k_hi[mine], k_mid[mine], k_lo[mine]
            head = chip * chip_heads + m
            stacked = jnp.concatenate([a, b, a, c, b, a], axis=0)
            scores = dot(q_cat[head], stacked) + bias_of(head)
            top = jnp.max(scores, axis=1, keepdims=True)
            expo = jnp.exp(scores - top)
            total = jnp.sum(expo, axis=1, keepdims=True)
            expos.append(expo)
            stat = jnp.where(head_lane == m, jnp.where(upper, total, top), stat)
        msg[chip, rows:] = stat
        for copy in msg_copies(chip, 1):
            copy.start()
        return halves(jnp.concatenate(expos, axis=0))

    def attend_values(t, u, expos):
        chip = chip_at(t, u)
        await_other(chip, 1)
        e_hi, e_lo = expos
        v_hi, v_lo = halves(v_buf[pl.ds(2 * chip, 2)].reshape(wide, cols))
        out = dot_nt(e_hi, v_hi) + (dot_nt(e_hi, v_lo) + dot_nt(e_lo, v_hi))
        part = out[:rows]
        for m in range(1, chip_heads):
            part = jnp.where(head_lane == m, out[m * rows : (m + 1) * rows], part)
        msg[chip, :rows] = part
        for copy in msg_copies(chip, 0):
            copy.start()

    def attend(t, u):
        attend_values(t, u, attend_keys(t, u))

    def combine(t, u):
        chip = chip_at(t, u)
        for copy in msg_copies(chip, 0) + msg_copies(chip, 1):
            copy.wait()
        every = [msg[chip]] + [msg_in[k, chip] for k in range(n_col - 1)]
        stats = [e[rows:] for e in every]
        down = [pltpu.roll(s, wide - head_dim // 2, 1) for s in stats]
        up = [pltpu.roll(s, head_dim // 2, 1) for s in stats]
        tops = [jnp.where(upper, r, s) for s, r in zip(stats, up)]
        totals = [jnp.where(upper, s, r) for s, r in zip(stats, down)]
        highest = functools.reduce(jnp.maximum, tops)
        scales = [jnp.exp(top - highest) for top in tops]
        total = sum(s * t for s, t in zip(scales, totals))
        attn = sum(e[:rows] * s for e, s in zip(every, scales)) / total
        a_hi, a_lo = halves(attn)
        at = pl.multiple_of(chip * wide, wide)
        w_hi, w_lo = halves(w_out_buf[pl.ds(at, wide), :])
        acc[...] += dot(a_hi, w_hi) + (dot(a_hi, w_lo) + dot(a_lo, w_hi))

    def stage(t):
        def one(u, carry):
            attend(t, u)
            if t:
                combine(t - 1, u)
            return carry

        lax.fori_loop(0, 2, one, 0)

    cut = (0, groups // 2, 5 * groups // 6, groups)
    lax.fori_loop(cut[0], cut[1], bias_group, 0)
    event(1, 0)
    lax.fori_loop(cut[1], cut[2], bias_group, 0)
    event(1, 1)
    lax.fori_loop(cut[2], cut[3], bias_group, 0)
    for k in range(1, n_col):
        source = lax.rem(col - k + n_col, n_col)
        q_copy(k - 1, source).wait_recv()
    lax.fori_loop(0, heads // tile_heads, spread_queries, 0)
    load_w_out.wait()
    event(2, 0)
    stage(0)
    event(2, 1)
    stage(1)
    for d in range(3, n_z):
        for kind in range(2):
            event(d, kind)
            attend(d - 1, kind)
            combine(d - 2, kind)
    attend(n_z - 1, 0)
    cross_sends(n_z - 1, 0, start, True)
    expos = attend_keys(n_z - 1, 1)
    for copy in sum_copies:
        copy.wait()
    cross_sends(n_z - 1, 1, start, True)
    attend_values(n_z - 1, 1, expos)
    for u in range(2):
        combine(n_z - 2, u)
    for u in range(2):
        combine(n_z - 1, u)

    seq_new = acc[...]
    seq_out[...] = seq_new
    local_mean = jnp.mean(seq_new, axis=1, keepdims=True)
    centred = seq_new - local_mean
    spread = jnp.sum(centred * centred, axis=1, keepdims=True)
    both_hi, both_lo = halves(both_t[...])
    c_hi, c_lo = halves(centred)
    packet[:rows] = dot_nt(c_hi, both_hi) + (dot_nt(c_hi, both_lo) + dot_nt(c_lo, both_hi))
    wide_lane = lax.broadcasted_iota(jnp.int32, (rows, 2 * proj), 1)
    packet[rows:] = jnp.where(wide_lane < proj, local_mean, spread)
    packets = [
        put(packet, packet_in.at[k], pack_send.at[k], pack_recv.at[k], {"col": peer})
        for k, peer in enumerate(col_peers)
    ]
    for copy in packets:
        copy.start()
    for copy in packets:
        copy.wait()
    every = [packet[...]] + [packet_in[k] for k in range(n_col - 1)]
    weights = [sums[:1]] + [sums_in[k, :1] for k in range(n_col - 1)]
    means = [p[rows:, :1] for p in every]
    mean = sum(means) / n_col
    offsets = [m - mean for m in means]
    variance = (
        sum(p[rows:, proj : proj + 1] for p in every) + here * sum(o * o for o in offsets)
    ) / width
    both = sum(p[:rows] + o * w for p, o, w in zip(every, offsets, weights))
    both = both * lax.rsqrt(variance + 1e-05)
    left_out[...] = both[:, :proj]
    half = rows // 2
    right_mine[...] = jnp.concatenate([both[:half, proj:], both[half:, proj:]], axis=1)

    mine = lax.div(row, blocks) == col
    own = lax.rem(row, blocks)

    def row_copies():
        return [
            put(
                right_mine, right_buf.at[own], right_send.at[k], right_recv.at[own],
                {"row": peer},
            )
            for k, peer in enumerate(row_peers)
        ]

    @pl.when(mine)
    def _():
        for copy in row_copies():
            copy.start()
        keep = pltpu.make_async_copy(right_mine, right_buf.at[own], right_recv.at[own])
        keep.start()
        keep.wait()

    def relay(j, block):
        slot = right_buf.at[block]
        return put(slot, slot, relay_send.at[j], right_recv.at[block], {"row": core_peer})

    for j in range(blocks // 2):
        block = 2 * j + core

        @pl.when(col * blocks + block != row)
        def _():
            relay(j, block).wait_recv()

        relay(j, block).start()
    for j in range(blocks // 2):
        relay(j, 2 * j + 1 - core).wait_recv()
    for b in range(blocks):
        packed = right_buf[b]
        right_out[b * rows : b * rows + half] = packed[:, :proj]
        right_out[b * rows + half : (b + 1) * rows] = packed[:, proj:]

    for j in range(blocks // 2):
        relay(j, 2 * j + core).wait_send()

    @pl.when(mine)
    def _():
        for copy in row_copies():
            copy.wait_send()

    for kind in range(2):
        own_sends(kind, wait_send)
        for d in range(1, n_z):
            line_sends(d, kind, wait_send, False)
        for d in range(n_z):
            cross_sends(d, kind, wait_send, False)
    for d in range(n_z):
        around_sends(d, wait_send, False)
    for k in range(n_col - 1):
        q_copy(k, col).wait_send()


def sequence_update(seq, query, key, value, pair, w_bias, w_out, w_left, w_right):
    n, n_col = lax.axis_size("row"), lax.axis_size("col")
    rows, cols, channels = pair.shape
    heads = w_bias.shape[1]
    feats = key.shape[1]
    width, here = w_out.shape
    head_dim = width // heads
    proj = w_left.shape[1]
    blocks = cols // rows
    group = 8
    peers = n_col - 1
    n_z = n // 4
    chips = n // 2
    any_space = pl.BlockSpec(memory_space=pl.ANY)
    vmem = pl.BlockSpec(memory_space=pltpu.VMEM)
    dma = pltpu.SemaphoreType.DMA
    return pl.pallas_call(
        functools.partial(sequence_kernel, n, n_col, head_dim, heads),
        out_shape=(
            jax.ShapeDtypeStruct(seq.shape, F32),
            jax.ShapeDtypeStruct((rows, proj), F32),
            jax.ShapeDtypeStruct((cols, proj), F32),
        ),
        in_specs=[any_space] * 4 + [vmem] + [any_space] * 4,
        out_specs=(vmem,) * 3,
        scratch_shapes=[
            pltpu.VMEM((n, feats, cols), F32),
            pltpu.VMEM((n, feats, cols), F32),
            pltpu.VMEM((n_col, rows, here), F32),
            pltpu.VMEM((heads, rows, 6 * head_dim), BF16),
            pltpu.VMEM((pl.cdiv(cols, LANES), heads * rows, LANES), F32),
            pltpu.VMEM((rows // group, group, cols, channels), F32),
            pltpu.VMEM((2 * heads, 2 * channels), BF16),
            pltpu.VMEM((width, here), F32),
            pltpu.VMEM((2 * proj, here), F32),
            pltpu.VMEM((rows, here), F32),
            pltpu.VMEM((chips, 2 * rows, 2 * feats), F32),
            pltpu.VMEM((peers, chips, 2 * rows, 2 * feats), F32),
            pltpu.VMEM((8, 2 * proj), F32),
            pltpu.VMEM((peers, 8, 2 * proj), F32),
            pltpu.VMEM((2 * rows, 2 * proj), F32),
            pltpu.VMEM((peers, 2 * rows, 2 * proj), F32),
            pltpu.VMEM((rows // 2, 2 * proj), F32),
            pltpu.VMEM((blocks, rows // 2, 2 * proj), F32),
            dma((n, 2)), dma((n_z, 2, 2)), dma((n_z, 2, 2)), dma((n_z, 2, 2, 2)),
            dma((n_z, 2)),
            dma((peers,)), dma((n_col,)), dma((rows // group,)), dma((4,)),
            dma((peers, chips, 2)), dma((peers, chips, 2)), dma((peers,)), dma((peers,)),
            dma((peers,)), dma((peers,)),
            dma((n // 2 - 1,)), dma((blocks,)), dma((blocks // 2,)),
        ],
        compiler_params=pltpu.CompilerParams(
            vmem_limit_bytes=VMEM_LIMIT, collective_id=0, has_side_effects=True
        ),
        name="sequence_update",
    )(key.T, value.T, query, pair, w_bias.T, seq, w_out, w_left.T, w_right.T)


def transition_kernel(
    pair_ref, left_ref, right_ref, w_outer_ref, bias_ref, w_up_ref, w_down_ref, seq_ref,
    seq_out, out_ref,
    left_t, right_s, left_d, up_ref, up8_ref, down_ref, down8_ref,
):
    step = pl.program_id(0)
    group, cols, channels = pair_ref.shape
    proj = left_ref.shape[1]
    dot = functools.partial(jnp.dot, preferred_element_type=F32)

    @pl.when(step == 0)
    def _():
        seq_out[...] = seq_ref[...]
        left = left_ref[...]
        left_t[...] = left.T
        left_d[...] = jnp.dot(left, w_outer_ref[proj:], precision=HIGH) + bias_ref[...]
        r_hi, r_lo = halves(right_ref[...])
        right_s[...] = jnp.concatenate([r_hi, r_lo, r_hi], axis=1)
        up = w_up_ref[...] * HIDDEN_SCALE
        up_hi = up.astype(BF16)
        up_ref[...] = jnp.concatenate([up_hi, up_hi], axis=0)
        up8_ref[...] = (up - up_hi.astype(F32)).astype(F8)
        down = w_down_ref[...] * (1.0 / HIDDEN_SCALE)
        down_hi, down_lo = halves(down)
        down_ref[...] = jnp.concatenate([down_hi, down_lo], axis=1)
        down8_ref[...] = (w_down_ref[...] * DOWN_SCALE).astype(F8)

    lane = lax.broadcasted_iota(jnp.int32, left_t.shape, 1)
    w_prod = w_outer_ref[:proj]
    w_diff = w_outer_ref[proj:]
    weights = []
    for g in range(group):
        column = jnp.sum(
            jnp.where(lane == step * group + g, left_t[...], 0.0), axis=1, keepdims=True
        )
        w_hi, w_lo = halves(column * w_prod - w_diff)
        weights.append(jnp.concatenate([w_hi, w_hi, w_lo], axis=0))
    outer = dot(right_s[...], jnp.concatenate(weights, axis=1))
    for first in range(0, group, 2):
        pick = range(first, first + 2)
        mids = [
            pair_ref[g]
            + (
                outer[:, g * channels : (g + 1) * channels]
                + left_d[pl.ds(step * group + g, 1), :]
            )
            for g in pick
        ]
        xs = [channel_norm(mid) for mid in mids]
        pairs = [jnp.concatenate(halves(x), axis=1) for x in xs]
        main = [dot(x, up_ref[...]) for x in pairs]
        rest = [dot(x.astype(F8), up8_ref[...]) for x in xs]
        hidden = [jnp.maximum(m + r, 0.0) for m, r in zip(main, rest)]
        highs = [h.astype(BF16) for h in hidden]
        lows = [(h - high.astype(F32)).astype(F8) for h, high in zip(hidden, highs)]
        both = [dot(high, down_ref[...]) for high in highs]
        rest = [dot(low, down8_ref[...]) * (1.0 / (HIDDEN_SCALE * DOWN_SCALE)) for low in lows]
        for g, mid, b, r in zip(pick, mids, both, rest):
            out_ref[g] = mid + (b[:, :channels] + (b[:, channels:] + r))


def transition(pair, left, right, w_outer, outer_bias, w_up, w_down, seq_new):
    rows, cols, channels = pair.shape
    proj = left.shape[1]
    hidden = w_up.shape[1]
    group = 4

    def whole(x):
        return pl.BlockSpec(x.shape, lambda i: (0,) * x.ndim)

    block = pl.BlockSpec((group, cols, channels), lambda i: (i, 0, 0))
    fixed = (left, right, w_outer, outer_bias.reshape(1, channels), w_up, w_down, seq_new)
    return pl.pallas_call(
        transition_kernel,
        out_shape=(
            jax.ShapeDtypeStruct(seq_new.shape, F32),
            jax.ShapeDtypeStruct(pair.shape, F32),
        ),
        grid=(rows // group,),
        in_specs=[block] + [whole(x) for x in fixed],
        out_specs=(whole(seq_new), block),
        scratch_shapes=[
            pltpu.VMEM((proj, rows), F32),
            pltpu.VMEM((cols, 3 * proj), BF16),
            pltpu.VMEM((rows, channels), F32),
            pltpu.VMEM((2 * channels, hidden), BF16),
            pltpu.VMEM((channels, hidden), F8),
            pltpu.VMEM((hidden, 2 * channels), BF16),
            pltpu.VMEM((hidden, channels), F8),
        ],
        compiler_params=pltpu.CompilerParams(vmem_limit_bytes=VMEM_LIMIT),
        name="transition",
    )(pair, *fixed)


def per_device(
    seq, query, key, value, pair, w_bias, w_out, w_left, w_right, w_outer, outer_bias, w_up, w_down
):
    seq_new, left, right = sequence_update(
        seq, query, key, value, pair, w_bias, w_out, w_left, w_right
    )
    return transition(pair, left, right, w_outer, outer_bias, w_up, w_down, seq_new)


def solution(mesh):
    in_specs = (
        P("row", "col"),
        P("row", "col"),
        P("col", "row"),
        P("col", "row"),
        P("row", "col", None),
        P(),
        P(None, "col"),
        P("col", None),
        P("col", None),
        P(),
        P(),
        P(),
        P(),
    )
    out_specs = (P("row", "col"), P("row", "col", None))
    return jax.shard_map(
        per_device, mesh=mesh, in_specs=in_specs, out_specs=out_specs, check_vma=False
    )
```
